256 devices in a mesh: rows: 16 (over y, x), cols: 8 (over z), depth: 2 (over core).
Axes of the slice: x: 4, y: 4, z: 8, core: 2. Of those that a mesh axis runs over, the one named last changes fastest.
Arguments:
- tile_left: float32 [16, 8, 64, 2048], P('rows', 'cols'), may hold values from -6 to 6
- tile_right: float32 [16, 8, 64, 2048], P('rows', 'cols'), may hold values from -0.75 to 0.75
- left_u: bfloat16 [2, 16, 16, 64, 2048], P('depth', 'cols', 'rows'), may hold values from -6 to 6
- left_v: bfloat16 [2, 16, 16, 64, 2048], P('depth', 'cols', 'rows'), may hold values from -0.0625 to 0.0625
- rank_left: int32 [2, 16, 16], P('depth', 'cols', 'rows'), may hold values from 16 to 64
- right_u: bfloat16 [2, 16, 8, 64, 2048], P('depth', 'rows', 'cols'), may hold values from -6 to 6
- right_v: bfloat16 [2, 16, 8, 64, 2048], P('depth', 'rows', 'cols'), may hold values from -0.0625 to 0.0625
- rank_right: int32 [2, 16, 8], P('depth', 'rows', 'cols'), may hold values from 16 to 64
- triples: int32 [16, 8, 2, 6], P('rows', 'cols', 'depth'), may hold values from -1 to 15, as said below
Outputs:
- new_left: float32 [16, 8, 64, 2048], P('rows', 'cols', None, 'depth')
- new_right: float32 [16, 8, 64, 2048], P('rows', 'cols', None, 'depth')
The draws below stay inside these ranges and needn't reach their ends.
Inputs may be any that keep to these rules, and one draw needn't show every extreme that they name: `triples`: for each tile and layer the first entries are distinct panel numbers of 0 to 15 and the remaining entries are -1; every list has at least one panel number, and in every draw some tile in some layer lists all 6.
All inputs are finite; a program needn't handle non-finite values.
Results may differ from the reference program's by a relative error of at most 0.0043.
Values may be sent and summed in bfloat16 or wider, within the bound.
No kernel may reach another device: no remote copies, remote signals or barrier semaphores. Data moves between devices by JAX's collectives and lax.ppermute only.
A program may use at most 128 MiB of HBM per device.

```python
import math
import jax
import jax.numpy as jnp
from jax import lax

NB = 2048
RK = 64
KL = 16
MAXA = 6
NTR = 16
NTC = 8
LAYERS = 2
N_DEPTH = 2


def draw_triples(key, part):
    keys = jax.random.split(jax.random.fold_in(key, 7), 4)
    total = NTR * NTC * LAYERS
    scores = jax.random.randint(keys[0], (total, KL), 0, 1 << 20) * KL + jnp.arange(KL, dtype=jnp.int32)[None, :]
    order = jnp.argsort(scores, axis=1).astype(jnp.int32)[:, :MAXA]
    first = jax.random.randint(keys[1], (total,), 0, MAXA)
    second = jax.random.randint(keys[2], (total,), 0, MAXA)
    counts = 1 + first * second // max(MAXA - 1, 1)
    spot = jax.random.randint(keys[3], (), 0, total)
    counts = jnp.where(jnp.arange(total) == spot, MAXA, counts)
    slots = jnp.arange(MAXA, dtype=jnp.int32)[None, :]
    listed = jnp.where(slots < counts[:, None], order, -1)
    return listed.astype(jnp.int32).reshape(NTR, NTC, LAYERS, MAXA)


def set_ends(result, key, least, top_value):
    longest = result.shape.index(max(result.shape))
    spots = []
    for shift in (0, 1):
        where = [jax.random.randint(jax.random.fold_in(key, axis), (), 0, length) for axis, length in enumerate(result.shape)]
        where[longest] = (where[longest] + shift) % result.shape[longest]
        spots.append(tuple(where))
    return result.at[spots[0]].set(least).at[spots[1]].set(top_value)


def block_scale(stream_key, shape, pieces, least, high):
    factor_of = 1.0
    for position, blocks in pieces:
        heights = jax.random.uniform(jax.random.fold_in(jax.random.fold_in(stream_key, 6), position), (blocks,), jnp.float32, least / len(pieces), high / len(pieces))
        factor_of = factor_of * jnp.repeat(jnp.exp(heights), shape[position] // blocks).reshape((-1,) + (1,) * (len(shape) - 1 - position))
    return factor_of


def bell_draw(stream_key, shape, deviation, reach, cuts=(), kind=jnp.bfloat16):
    array = jax.random.normal(stream_key, shape, jnp.float32) * deviation
    if len(cuts) > 0:
        array = block_scale(stream_key, shape, cuts, -0.22, 0.18) * array
    return jnp.clip(array, min=-reach, max=reach).astype(kind)


def setup_inputs(seed: int = 0) -> dict:
    arg_keys = jax.random.split(jax.random.key(seed), 10)
    tile_left = bell_draw(arg_keys[0], (NTR, NTC, RK, NB), 1.0, 6.0, ((0, 16), (1, 8)), jnp.float32)
    tile_right = bell_draw(arg_keys[1], (NTR, NTC, RK, NB), 0.125, 0.75, ((0, 16), (1, 8)), jnp.float32)
    left_u = bell_draw(arg_keys[2], (LAYERS, KL, NTR, RK, NB), 1.0, 6.0, ((0, 2), (1, 8), (2, 16)))
    left_v = bell_draw(arg_keys[3], (LAYERS, KL, NTR, RK, NB), (NB * RK // 16) ** -0.5, 0.0625, ((0, 2), (1, 8), (2, 16)))
    rank_left = set_ends(jax.random.randint(arg_keys[4], (LAYERS, KL, NTR), RK // 4, RK + 1), jax.random.fold_in(arg_keys[4], 1), RK // 4, RK).astype(jnp.int32)
    right_u = bell_draw(arg_keys[5], (LAYERS, KL, NTC, RK, NB), 1.0, 6.0, ((0, 2), (1, 16), (2, 8)))
    right_v = bell_draw(arg_keys[6], (LAYERS, KL, NTC, RK, NB), (NB * RK // 16) ** -0.5, 0.0625, ((0, 2), (1, 16), (2, 8)))
    rank_right = set_ends(jax.random.randint(arg_keys[7], (LAYERS, KL, NTC), RK // 4, RK + 1), jax.random.fold_in(arg_keys[7], 1), RK // 4, RK).astype(jnp.int32)
    triples = draw_triples(jax.random.fold_in(arg_keys[9], 71), 0)
    return {"tile_left": tile_left, "tile_right": tile_right, "left_u": left_u, "left_v": left_v, "rank_left": rank_left, "right_u": right_u, "right_v": right_v, "rank_right": rank_right, "triples": triples}


HIGHEST = lax.Precision.HIGHEST

def cross(first, second, dim_first, dim_second):
    return lax.dot_general(first.astype(jnp.float32), second.astype(jnp.float32), (((dim_first,), (dim_second,)), ((), ())), precision=HIGHEST, preferred_element_type=jnp.float32)

def start_rows(rank, width):
    freq = lax.broadcasted_iota(jnp.int32, (rank, width), 0) + 1
    cell = 2 * lax.broadcasted_iota(jnp.int32, (rank, width), 1) + 1
    phase = freq * cell % (4 * width)
    return jnp.cos(phase.astype(jnp.float32) * (math.pi / (2 * width)))

def orthonormal(rows_t):
    gram = cross(rows_t, rows_t, 1, 1)
    shift = 1e-05 * jnp.trace(gram) / gram.shape[0] + 1e-06
    gram = gram + shift * jnp.eye(gram.shape[0], dtype=gram.dtype)
    lower = lax.linalg.cholesky(gram)
    return lax.linalg.triangular_solve(lower, rows_t, left_side=True, lower=True)

def compress(left_t, right_t):
    probe = start_rows(RK, NB)
    for sweep in range(2):
        first = cross(left_t, probe, 1, 1)
        image = orthonormal(cross(first, right_t, 0, 0))
        second = cross(right_t, image, 1, 1)
        probe = orthonormal(cross(second, left_t, 0, 0))
    first = cross(left_t, probe, 1, 1)
    return (probe, cross(first, right_t, 0, 0))

def slot_term(outer_left, inner_left, rank_l, inner_right, rank_r):
    inner = lax.dot_general(inner_left.astype(jnp.float32), inner_right.astype(jnp.float32), (((1,), (1,)), ((), ())), preferred_element_type=jnp.float32)
    index = jnp.arange(RK)
    keep = (index[:, None] < rank_l) & (index[None, :] < rank_r)
    inner = jnp.where(keep, inner, 0.0).astype(jnp.bfloat16)
    return lax.dot_general(inner.astype(jnp.float32), outer_left.astype(jnp.float32), (((0,), (0,)), ((), ())), preferred_element_type=jnp.float32)

def reference(tile_left, tile_right, left_u, left_v, rank_left, right_u, right_v, rank_right, triples):

    def one_tile(flat):
        row = flat // NTC
        col = flat % NTC
        results = []
        for layer in range(N_DEPTH):
            terms = [tile_left[row, col] / N_DEPTH]
            bases = [tile_right[row, col]]
            for slot in range(MAXA):
                panel = triples[row, col, layer, slot]
                valid = panel >= 0
                chosen = jnp.maximum(panel, 0)
                term = slot_term(left_u[layer, chosen, row], left_v[layer, chosen, row], rank_left[layer, chosen, row], right_v[layer, chosen, col], rank_right[layer, chosen, col])
                terms.append(jnp.where(valid, -term, 0.0))
                bases.append(jnp.where(valid, right_u[layer, chosen, col].astype(jnp.float32), 0.0))
            results.append(compress(jnp.concatenate(terms, axis=0), jnp.concatenate(bases, axis=0)))
        while len(results) > 1:
            joined = []
            for pair in range(len(results) // 2):
                lower_item = results[2 * pair]
                upper_item = results[2 * pair + 1]
                joined.append(compress(jnp.concatenate([lower_item[0], upper_item[0]], axis=0), jnp.concatenate([lower_item[1], upper_item[1]], axis=0)))
            results = joined
        probe, image = results[0]
        return (probe * math.sqrt(NB), image / math.sqrt(NB))
    lefts, rights = lax.map(one_tile, jnp.arange(NTR * NTC))
    return (lefts.reshape(NTR, NTC, RK, NB), rights.reshape(NTR, NTC, RK, NB))
```

```python
import math

import jax
import jax.numpy as jnp
from jax import lax
from jax.experimental import pallas as pl
from jax.experimental.pallas import tpu as pltpu
from jax.sharding import PartitionSpec as P

NB = 2048
RK = 64
BF = jnp.bfloat16
F32 = jnp.float32


def nt(first, second):
    return lax.dot_general(
        first, second, (((1,), (1,)), ((), ())), preferred_element_type=F32
    )


def nn(first, second):
    return lax.dot_general(
        first, second, (((1,), (0,)), ((), ())), preferred_element_type=F32
    )


def halves(x):
    high = x.astype(BF)
    return high, (x - high.astype(F32)).astype(BF)


def start_pair():
    rows = start_rows(RK, NB)
    high = lax.reduce_precision(rows, 8, 7)
    return jnp.concatenate([high, rows - high], axis=0).astype(BF)


def product(mul, first, second):
    a, b = halves(first), halves(second)
    return mul(a[0], b[0]) + (mul(a[0], b[1]) + mul(a[1], b[0]))


def start_rows(rank, width):
    freq = lax.broadcasted_iota(jnp.int32, (rank, width), 0) + 1
    cell = 2 * lax.broadcasted_iota(jnp.int32, (rank, width), 1) + 1
    phase = freq * cell % (4 * width)
    return jnp.cos(phase.astype(F32) * (math.pi / (2 * width)))


def spread(x, lane):
    return jnp.broadcast_to(x[:, lane : lane + 1], (8, 128))


def factor_inverse(full):
    v = [full[8 * b : 8 * b + 8] for b in range(8)]
    sub = lax.broadcasted_iota(jnp.int32, (8, 128), 0)
    out = []
    for b in range(8):
        at = 8 * b
        rows = [jnp.broadcast_to(v[b][p : p + 1], (8, 128)) for p in range(8)]
        s = [[spread(rows[p], at + q) for q in range(p + 1)] for p in range(8)]
        low = [[None] * 8 for _ in range(8)]
        n, inv = [], []
        for p in range(8):
            d = s[p][p]
            y = lax.rsqrt(d)
            y = y * (1.5 - 0.5 * d * y * y)
            inv.append(y)
            n.append(rows[p] * y)
            for q in range(p + 1, 8):
                low[q][p] = s[q][p] * y
            for q in range(p + 1, 8):
                for r in range(p + 1, q + 1):
                    s[q][r] = s[q][r] - low[q][p] * low[r][p]
                rows[q] = rows[q] - low[q][p] * n[p]
        block = n[0]
        for p in range(1, 8):
            block = jnp.where(sub == p, n[p], block)
        out.append(block)
        if b < 7:
            t = [None] * 8
            for q in reversed(range(8)):
                acc = n[q]
                for p in range(q + 1, 8):
                    acc = acc - low[p][q] * t[p]
                t[q] = acc * inv[q]
            for below in range(b + 1, 8):
                acc = v[below]
                for q in range(8):
                    acc = acc - spread(v[below], at + q) * t[q]
                v[below] = acc
    return jnp.concatenate(out, axis=0)


def masks():
    row = lax.broadcasted_iota(jnp.int32, (RK, 2 * RK), 0)
    col = lax.broadcasted_iota(jnp.int32, (RK, 2 * RK), 1)
    return row == col, row + RK == col, col >= RK


def sweeps(left_gram, right_gram, z):
    diag, unit, upper = masks()
    n = z.shape[1]
    gz = product(nn, z, right_gram)
    for half in range(4):
        after = left_gram if half % 2 == 0 else right_gram
        gram = product(nt, z, jnp.concatenate([gz, jnp.zeros((RK, n), F32)], axis=0))
        trace = jnp.sum(jnp.where(diag, gram, 0.0), keepdims=True)
        shift = 1e-05 * trace / RK + 1e-06
        full = jnp.where(diag, gram + shift, gram)
        full = jnp.where(unit, 1.0, full)
        if half < 3:
            ahead = product(nn, gz, after)
        inverse = jnp.where(upper, factor_inverse(full), 0.0)
        if half < 3:
            both = jnp.concatenate([gz, ahead], axis=1)
            both = product(nn, inverse, jnp.concatenate([both, both], axis=0))
            z, gz = both[:, :n], both[:, n:]
        else:
            both = jnp.concatenate([z, gz], axis=1)
            both = product(nn, inverse, jnp.concatenate([both, both], axis=0))
            return both[:, :n], both[:, n:]


def layer_kernel(
    triples, tile_left, tile_right, inner, start, left_u, right_u, probe, image, w, r, d, sems
):
    copies = []
    for slot in range(6):
        chosen = jnp.maximum(triples[slot], 0)
        for side, (src, dst) in enumerate(((left_u, w), (right_u, r))):
            copy = pltpu.make_async_copy(
                src.at[chosen], dst.at[pl.ds(RK * slot, RK)], sems.at[side, slot]
            )
            copy.start()
            copies.append(copy)
    w[384:448], w[448:512] = halves(tile_left[...])
    r[384:448], r[448:512] = halves(tile_right[...])
    row = lax.broadcasted_iota(jnp.int32, (128, 128), 0)
    col = lax.broadcasted_iota(jnp.int32, (128, 128), 1)
    d[...] = jnp.zeros_like(d)
    for slot in range(6):
        panel = triples[slot]
        value = -inner[jnp.maximum(panel, 0)]
        value = jnp.where(panel >= 0, value, jnp.zeros_like(value))
        at = RK * (slot % 2)
        d[slot // 2, at : at + RK, at : at + RK] = value
    d[3] = jnp.where((row - col) % RK == 0, 0.5, 0.0).astype(BF)
    for copy in copies:
        copy.wait()
    left = w[...]
    right = r[...]
    right_gram = nt(right, right)
    raw = nt(left, left)
    z = nt(start[...], left)
    z = z[:RK] + z[RK:]
    mixed = []
    for t in range(4):
        high, low = halves(raw[128 * t : 128 * t + 128])
        mixed.append(nn(d[t], high) + nn(d[t], low))
    mixed = jnp.concatenate(mixed + [z], axis=0)
    high, low = halves(mixed)
    out = []
    for t in range(4):
        cut = slice(128 * t, 128 * t + 128)
        out.append(nt(high[:, cut], d[t]) + nt(low[:, cut], d[t]))
    out = jnp.concatenate(out, axis=1)
    x, y = sweeps(out[:512], right_gram, out[512:])
    high, low = halves(x)
    out = []
    for t in range(4):
        cut = slice(128 * t, 128 * t + 128)
        out.append(nn(high[:, cut], d[t]) + nn(low[:, cut], d[t]))
    high, low = halves(jnp.concatenate(out, axis=1))
    probe[...] = nn(high, left) + nn(low, left)
    high, low = halves(y)
    image[...] = nn(high, right) + nn(low, right)


def layer_update(triples, tile_left, tile_right, inner, start, left_u, right_u):
    vmem = pl.BlockSpec(memory_space=pltpu.VMEM)
    hbm = pl.BlockSpec(memory_space=pl.ANY)
    return pl.pallas_call(
        layer_kernel,
        out_shape=[jax.ShapeDtypeStruct((RK, NB), F32)] * 2,
        in_specs=[pl.BlockSpec(memory_space=pltpu.SMEM), vmem, vmem, vmem, vmem, hbm, hbm],
        out_specs=[vmem, vmem],
        scratch_shapes=[
            pltpu.VMEM((512, NB), BF),
            pltpu.VMEM((512, NB), BF),
            pltpu.VMEM((4, 128, 128), BF),
            pltpu.SemaphoreType.DMA((2, 6)),
        ],
        compiler_params=pltpu.CompilerParams(vmem_limit_bytes=40 << 20),
        name="layer_update",
    )(triples, tile_left, tile_right, inner, start, left_u, right_u)


def join_kernel(offset, probes_a, probes_b, images_a, images_b, start, new_left, new_right, w, r):
    for store, first, second in ((w, probes_a, probes_b), (r, images_a, images_b)):
        store[0:64], store[128:192] = halves(first[...])
        store[64:128], store[192:256] = halves(second[...])

    def folded(x):
        return (x[:128, :128] + x[128:, 128:]) + (x[:128, 128:] + x[128:, :128])

    left = w[...]
    right = r[...]
    z = nt(start[...], left)
    z = z[:RK] + z[RK:]
    z = z[:, :128] + z[:, 128:]
    x, y = sweeps(folded(nt(left, left)), folded(nt(right, right)), z)
    share = new_left.shape[1]
    cut = pl.ds(pl.multiple_of(offset[0], share), share)
    for store, coefs, out, scale in (
        (w, x, new_left, math.sqrt(NB)),
        (r, y, new_right, 1.0 / math.sqrt(NB)),
    ):
        high, low = halves(coefs)
        out[...] = scale * (
            nn(high, store[0:128, cut])
            + (nn(high, store[128:256, cut]) + nn(low, store[0:128, cut]))
        )


def join(offset, probes_a, probes_b, images_a, images_b, start, share):
    vmem = pl.BlockSpec(memory_space=pltpu.VMEM)
    return pl.pallas_call(
        join_kernel,
        out_shape=[jax.ShapeDtypeStruct((RK, share), F32)] * 2,
        in_specs=[pl.BlockSpec(memory_space=pltpu.SMEM)] + [vmem] * 5,
        out_specs=[vmem, vmem],
        scratch_shapes=[pltpu.VMEM((256, NB), BF), pltpu.VMEM((256, NB), BF)],
        compiler_params=pltpu.CompilerParams(vmem_limit_bytes=40 << 20),
        name="join",
    )(offset, probes_a, probes_b, images_a, images_b, start)


def gathered(left_u, right_u):
    return (
        lax.all_gather(left_u, "cols", axis=0, tiled=True),
        lax.all_gather(right_u, "rows", axis=0, tiled=True),
    )


def inners(left_v, rank_left, right_v, rank_right):
    index = lax.broadcasted_iota(jnp.int32, (RK, 1), 0)
    left_v = jnp.where(index[None] < rank_left[:, None, None], left_v, 0)
    right_v = jnp.where(index < rank_right[0], right_v, 0)
    route = []
    for r in range(16):
        for c in range(8):
            route.append((r * 8 + c, ((r % 2) * 8 + c) * 8 + r // 2))
    right_v = lax.ppermute(right_v, ("rows", "cols"), route)
    right_v = lax.all_gather(right_v, "rows").reshape(2, 8 * RK, NB)
    inner = lax.dot_general(
        right_v, left_v, (((2,), (2,)), ((0,), (0,))), preferred_element_type=F32
    ).astype(BF)
    inner = inner.reshape(2, 8, RK, RK).transpose(1, 0, 2, 3)
    return lax.all_to_all(inner, "cols", 0, 0).reshape(16, RK, RK)


def shards(tile_left, tile_right, left_u, left_v, rank_left, right_u, right_v, rank_right, triples):
    inner = inners(left_v[0, :, 0], rank_left[0, :, 0], right_v[0, 0, 0], rank_right[0, 0])
    row_u, col_u = gathered(left_u[0, :, 0], right_u[0, :, 0])
    start = start_pair()
    probe, image = layer_update(
        triples[0, 0, 0], tile_left[0, 0], tile_right[0, 0], inner, start, row_u, col_u
    )
    layer = lax.axis_index("depth")
    other_probe, other_image = lax.ppermute((probe, image), "depth", [(0, 1), (1, 0)])
    share = NB // 2
    lower = layer == 0
    new_left, new_right = join(
        (layer * share).astype(jnp.int32).reshape(1),
        jnp.where(lower, probe, other_probe),
        jnp.where(lower, other_probe, probe),
        jnp.where(lower, image, other_image),
        jnp.where(lower, other_image, image),
        start,
        share,
    )
    return new_left.reshape(1, 1, RK, share), new_right.reshape(1, 1, RK, share)


def solution(mesh):
    in_specs = (
        P("rows", "cols", None, None),
        P("rows", "cols", None, None),
        P("depth", "cols", "rows", None, None),
        P("depth", "cols", "rows", None, None),
        P("depth", "cols", "rows"),
        P("depth", "rows", "cols", None, None),
        P("depth", "rows", "cols", None, None),
        P("depth", "rows", "cols"),
        P("rows", "cols", "depth", None),
    )
    out_specs = (P("rows", "cols", None, "depth"), P("rows", "cols", None, "depth"))
    return jax.shard_map(shards, mesh=mesh, in_specs=in_specs, out_specs=out_specs, check_vma=False)
```

```python
import math

import jax
import jax.numpy as jnp
from jax import lax
from jax.experimental import pallas as pl
from jax.experimental.pallas import tpu as pltpu
from jax.sharding import PartitionSpec as P

NB = 2048
RK = 64
BF = jnp.bfloat16
F32 = jnp.float32


def nt(first, second):
    return lax.dot_general(
        first, second, (((1,), (1,)), ((), ())), preferred_element_type=F32
    )


def nn(first, second):
    return lax.dot_general(
        first, second, (((1,), (0,)), ((), ())), preferred_element_type=F32
    )


def halves(x):
    high = x.astype(BF)
    return high, (x - high.astype(F32)).astype(BF)


def start_pair():
    rows = start_rows(RK, NB)
    high = lax.reduce_precision(rows, 8, 7)
    return jnp.concatenate([high, rows - high], axis=0).astype(BF)


def product(mul, first, second):
    a, b = halves(first), halves(second)
    return mul(a[0], b[0]) + (mul(a[0], b[1]) + mul(a[1], b[0]))


def start_rows(rank, width):
    freq = lax.broadcasted_iota(jnp.int32, (rank, width), 0) + 1
    cell = 2 * lax.broadcasted_iota(jnp.int32, (rank, width), 1) + 1
    phase = freq * cell % (4 * width)
    return jnp.cos(phase.astype(F32) * (math.pi / (2 * width)))


def spread(x, lane):
    return jnp.broadcast_to(x[:, lane : lane + 1], (8, 128))


def factor_inverse(full):
    v = [full[8 * b : 8 * b + 8] for b in range(8)]
    sub = lax.broadcasted_iota(jnp.int32, (8, 128), 0)
    out = []
    for b in range(8):
        at = 8 * b
        rows = [jnp.broadcast_to(v[b][p : p + 1], (8, 128)) for p in range(8)]
        s = [[spread(rows[p], at + q) for q in range(p + 1)] for p in range(8)]
        low = [[None] * 8 for _ in range(8)]
        n, inv = [], []
        for p in range(8):
            d = s[p][p]
            y = lax.rsqrt(d)
            y = y * (1.5 - 0.5 * d * y * y)
            inv.append(y)
            n.append(rows[p] * y)
            for q in range(p + 1, 8):
                low[q][p] = s[q][p] * y
            for q in range(p + 1, 8):
                for r in range(p + 1, q + 1):
                    s[q][r] = s[q][r] - low[q][p] * low[r][p]
                rows[q] = rows[q] - low[q][p] * n[p]
        block = n[0]
        for p in range(1, 8):
            block = jnp.where(sub == p, n[p], block)
        out.append(block)
        if b < 7:
            t = [None] * 8
            for q in reversed(range(8)):
                acc = n[q]
                for p in range(q + 1, 8):
                    acc = acc - low[p][q] * t[p]
                t[q] = acc * inv[q]
            for below in range(b + 1, 8):
                acc = v[below]
                for q in range(8):
                    acc = acc - spread(v[below], at + q) * t[q]
                v[below] = acc
    return jnp.concatenate(out, axis=0)


def masks():
    row = lax.broadcasted_iota(jnp.int32, (RK, 2 * RK), 0)
    col = lax.broadcasted_iota(jnp.int32, (RK, 2 * RK), 1)
    return row == col, row + RK == col, col >= RK


def store_gram(grams, at, gram):
    grams[0, at], grams[1, at] = halves(gram)


def gram_product(rows, grams, at):
    high, low = halves(rows)
    return nn(high, grams[0, at]) + (nn(high, grams[1, at]) + nn(low, grams[0, at]))


def inverse_rows(z, gz):
    diag, unit, upper = masks()
    gram = product(nt, z, jnp.concatenate([gz, jnp.zeros(gz.shape, F32)], axis=0))
    trace = jnp.sum(jnp.where(diag, gram, 0.0), keepdims=True)
    shift = 1e-05 * trace / RK + 1e-06
    full = jnp.where(diag, gram + shift, gram)
    full = jnp.where(unit, 1.0, full)
    return jnp.where(upper, factor_inverse(full), 0.0)


def sweeps(grams, z, z_ref, gz_ref):
    n = z.shape[1]
    z_ref[...] = z
    gz_ref[...] = gram_product(z, grams, 1)

    @pl.loop(0, 3)
    def _(half):
        z, gz = z_ref[...], gz_ref[...]
        ahead = gram_product(gz, grams, half % 2)
        both = jnp.concatenate([gz, ahead], axis=1)
        both = product(nn, inverse_rows(z, gz), jnp.concatenate([both, both], axis=0))
        z_ref[...] = both[:, :n]
        gz_ref[...] = both[:, n:]

    z, gz = z_ref[...], gz_ref[...]
    both = jnp.concatenate([z, gz], axis=1)
    both = product(nn, inverse_rows(z, gz), jnp.concatenate([both, both], axis=0))
    return both[:, :n], both[:, n:]


def take(choice, copies):
    for holds, sources in choice:

        @pl.when(holds)
        def _():
            for src, (dst, sem) in zip(sources, copies):
                pltpu.make_async_copy(src, dst, sem).start()


def right_choice(pieces, first, second):
    block = jnp.where(first == 0, 0, jnp.where(first == 3, 1, first + 1))
    own, before, after, far_low, far_high = pieces
    low = block < 2
    found = [
        (second == 0, own.at[block]),
        (second == 3, before.at[block]),
        (second == 1, after.at[block]),
        ((second == 2) & low, far_low.at[jnp.minimum(block, 1)]),
        ((second == 2) & (block >= 2), far_high.at[jnp.maximum(block, 2) - 2]),
    ]
    return [(holds, [src.at[pl.ds(0, 32)], src.at[pl.ds(32, 32)]]) for holds, src in found]


def left_choice(pieces, more, panel, col):
    offset = (panel // 2 - col + 8) % 8
    spot = panel % 2
    found = []
    for number, o in ((0, 0), (1, 1), (2, 2), (3, 3), (4, 5), (5, 6), (6, 7)):
        found.append((offset == o, [pieces[number].at[spot], more[number].at[spot]]))
    for number in (7, 8):
        holds = (offset == 4) & (spot == number - 7)
        found.append((holds, [pieces[number].at[0], more[number].at[0]]))
    return found


def layer_kernel(triples, place, tile_left, tile_right, start, *refs):
    left_u, left_v, pieces_a, pieces_b = refs[:9], refs[9:18], refs[18:23], refs[23:28]
    probe, image, w, r, inner_l, inner_r, d, first_left, first_right, begin = refs[28:38]
    grams, z_ref, gz_ref, sems = refs[38:]
    fixed = [
        pltpu.make_async_copy(src, dst, sems.at[6, n])
        for n, (src, dst) in enumerate(
            ((tile_left, first_left), (tile_right, first_right), (start, begin))
        )
    ]
    for copy in fixed:
        copy.start()
    place_x, place_y, col = place[0], place[1], place[2]
    waits = []
    for slot in range(6):
        panel = jnp.maximum(triples[slot], 0)
        at = RK * slot
        copies = [
            (w.at[pl.ds(at, RK)], sems.at[0, slot]),
            (inner_l.at[slot], sems.at[1, slot]),
        ]
        take(left_choice(left_u, left_v, panel, col), copies)
        waits += [(left_u[0].at[0], dst, sem) for dst, sem in copies]
        dx = (panel % 4 - place_x + 4) % 4
        dy = (panel // 4 - place_y + 4) % 4
        for half, (pieces, first, second) in enumerate(((pieces_a, dx, dy), (pieces_b, dy, dx))):
            more = 32 * half
            copies = [
                (r.at[pl.ds(at + more, 32)], sems.at[2 + 2 * half, slot]),
                (inner_r.at[slot, pl.ds(more, 32)], sems.at[3 + 2 * half, slot]),
            ]
            take(right_choice(pieces, first, second), copies)
            waits += [(pieces[0].at[0, pl.ds(0, 32)], dst, sem) for dst, sem in copies]
    for copy in fixed:
        copy.wait()
    w[384:448], w[448:512] = halves(first_left[...])
    r[384:448], r[448:512] = halves(first_right[...])
    row = lax.broadcasted_iota(jnp.int32, (128, 128), 0)
    col = lax.broadcasted_iota(jnp.int32, (128, 128), 1)
    d[...] = jnp.zeros_like(d)
    d[3] = jnp.where((row - col) % RK == 0, 0.5, 0.0).astype(BF)
    for src, dst, sem in waits:
        pltpu.make_async_copy(src, dst, sem).wait()
    for slot in range(6):
        value = -nt(inner_r[slot], inner_l[slot])
        value = jnp.where(triples[slot] >= 0, value, jnp.zeros_like(value)).astype(BF)
        at = RK * (slot % 2)
        d[slot // 2, at : at + RK, at : at + RK] = value
    left = w[...]
    right = r[...]
    store_gram(grams, 1, nt(right, right))
    raw = nt(left, left)
    z = nt(begin[...], left)
    z = z[:RK] + z[RK:]
    mixed = []
    for t in range(4):
        high, low = halves(raw[128 * t : 128 * t + 128])
        mixed.append(nn(d[t], high) + nn(d[t], low))
    mixed = jnp.concatenate(mixed + [z], axis=0)
    high, low = halves(mixed)
    out = []
    for t in range(4):
        cut = slice(128 * t, 128 * t + 128)
        out.append(nt(high[:, cut], d[t]) + nt(low[:, cut], d[t]))
    out = jnp.concatenate(out, axis=1)
    store_gram(grams, 0, out[:512])
    x, y = sweeps(grams, out[512:], z_ref, gz_ref)
    high, low = halves(x)
    out = []
    for t in range(4):
        cut = slice(128 * t, 128 * t + 128)
        out.append(nn(high[:, cut], d[t]) + nn(low[:, cut], d[t]))
    high, low = halves(jnp.concatenate(out, axis=1))
    probe[...] = nn(high, left) + nn(low, left)
    high, low = halves(y)
    image[...] = nn(high, right) + nn(low, right)


def layer_update(triples, place, *arrays):
    smem = pl.BlockSpec(memory_space=pltpu.SMEM)
    vmem = pl.BlockSpec(memory_space=pltpu.VMEM)
    hbm = pl.BlockSpec(memory_space=pltpu.HBM)
    return pl.pallas_call(
        layer_kernel,
        out_shape=[jax.ShapeDtypeStruct((RK, NB), F32)] * 2,
        in_specs=[smem, smem] + [hbm] * len(arrays),
        out_specs=[vmem, vmem],
        scratch_shapes=[
            pltpu.VMEM((512, NB), BF),
            pltpu.VMEM((512, NB), BF),
            pltpu.VMEM((6, RK, NB), BF),
            pltpu.VMEM((6, RK, NB), BF),
            pltpu.VMEM((4, 128, 128), BF),
            pltpu.VMEM((RK, NB), F32),
            pltpu.VMEM((RK, NB), F32),
            pltpu.VMEM((2 * RK, NB), BF),
            pltpu.VMEM((2, 2, 512, 512), BF),
            pltpu.VMEM((RK, 512), F32),
            pltpu.VMEM((RK, 512), F32),
            pltpu.SemaphoreType.DMA((7, 6)),
        ],
        compiler_params=pltpu.CompilerParams(vmem_limit_bytes=40 << 20),
        name="layer_update",
    )(triples, place, *arrays)


def join_kernel(
    offset, probes_a, probes_b, images_a, images_b, start, new_left, new_right, w, r, grams, z_ref, gz_ref
):
    for store, first, second in ((w, probes_a, probes_b), (r, images_a, images_b)):
        store[0:64], store[128:192] = halves(first[...])
        store[64:128], store[192:256] = halves(second[...])

    def folded(x):
        return (x[:128, :128] + x[128:, 128:]) + (x[:128, 128:] + x[128:, :128])

    left = w[...]
    right = r[...]
    z = nt(start[...], left)
    z = z[:RK] + z[RK:]
    z = z[:, :128] + z[:, 128:]
    store_gram(grams, 0, folded(nt(left, left)))
    store_gram(grams, 1, folded(nt(right, right)))
    x, y = sweeps(grams, z, z_ref, gz_ref)
    share = new_left.shape[1]
    cut = pl.ds(pl.multiple_of(offset[0], share), share)
    for store, coefs, out, scale in (
        (w, x, new_left, math.sqrt(NB)),
        (r, y, new_right, 1.0 / math.sqrt(NB)),
    ):
        high, low = halves(coefs)
        out[...] = scale * (
            nn(high, store[0:128, cut])
            + (nn(high, store[128:256, cut]) + nn(low, store[0:128, cut]))
        )


def join(offset, probes_a, probes_b, images_a, images_b, start, share):
    vmem = pl.BlockSpec(memory_space=pltpu.VMEM)
    return pl.pallas_call(
        join_kernel,
        out_shape=[jax.ShapeDtypeStruct((RK, share), F32)] * 2,
        in_specs=[pl.BlockSpec(memory_space=pltpu.SMEM)] + [vmem] * 5,
        out_specs=[vmem, vmem],
        scratch_shapes=[
            pltpu.VMEM((256, NB), BF),
            pltpu.VMEM((256, NB), BF),
            pltpu.VMEM((2, 2, 128, 128), BF),
            pltpu.VMEM((RK, 128), F32),
            pltpu.VMEM((RK, 128), F32),
        ],
        compiler_params=pltpu.CompilerParams(vmem_limit_bytes=40 << 20),
        name="join",
    )(offset, probes_a, probes_b, images_a, images_b, start)


def move(x, dx, dy):
    route = []
    for r in range(16):
        y, x_at = divmod(r, 4)
        route.append((r, (y + dy) % 4 * 4 + (x_at + dx) % 4))
    return lax.ppermute(x, "rows", route)


def turn(x, step):
    return lax.ppermute(x, "cols", [(c, (c + step) % 8) for c in range(8)])


def line(x, along_x):
    step = (lambda k: move(x, k, 0)) if along_x else (lambda k: move(x, 0, k))
    return jnp.stack([x, step(1), step(-1), step(2)])


def plane(stack, along_x):
    step = (lambda v, k: move(v, k, 0)) if along_x else (lambda v, k: move(v, 0, k))
    before, after = step(stack, 1), step(stack, -1)
    return [stack, before, after, step(before[:2], 1), step(after[2:], -1)]


def ring(own):
    f1, b1 = turn(own, 1), turn(own, -1)
    f2, b2 = turn(f1, 1), turn(b1, -1)
    f3, b3 = turn(f2, 1), turn(b2, -1)
    f4, b4 = turn(f3[:1], 1), turn(b3[1:], -1)
    return [own, b1, b2, b3, f3, f2, f1, f4, b4]


def masked(rows, rank):
    index = lax.broadcasted_iota(jnp.int32, (RK, 1), 0)
    return jnp.where(index < rank, rows, 0)


def shards(tile_left, tile_right, left_u, left_v, rank_left, right_u, right_v, rank_right, triples):
    row = lax.axis_index("rows")
    place = jnp.stack([row % 4, row // 4, lax.axis_index("cols")]).astype(jnp.int32)
    right_u = right_u[0, 0, 0]
    right_v = masked(right_v[0, 0, 0], rank_right[0, 0, 0])
    left_v = masked(left_v[0, :, 0], rank_left[0, :, 0][:, None, None])
    all_u = ring(left_u[0, :, 0])
    all_v = ring(left_v)
    half_a = line(jnp.concatenate([right_u[:32], right_v[:32]], axis=0), True)
    half_b = line(jnp.concatenate([right_u[32:], right_v[32:]], axis=0), False)
    pieces = plane(half_a, False) + plane(half_b, True)
    start = start_pair()
    probe, image = layer_update(
        triples[0, 0, 0], place, tile_left[0, 0], tile_right[0, 0], start, *all_u, *all_v, *pieces
    )
    layer = lax.axis_index("depth")
    other_probe, other_image = lax.ppermute((probe, image), "depth", [(0, 1), (1, 0)])
    share = NB // 2
    new_left, new_right = join(
        (layer * share).astype(jnp.int32).reshape(1),
        probe,
        other_probe,
        image,
        other_image,
        start,
        share,
    )
    return new_left.reshape(1, 1, RK, share), new_right.reshape(1, 1, RK, share)


def solution(mesh):
    in_specs = (
        P("rows", "cols", None, None),
        P("rows", "cols", None, None),
        P("depth", "cols", "rows", None, None),
        P("depth", "cols", "rows", None, None),
        P("depth", "cols", "rows"),
        P("depth", "rows", "cols", None, None),
        P("depth", "rows", "cols", None, None),
        P("depth", "rows", "cols"),
        P("rows", "cols", "depth", None),
    )
    out_specs = (P("rows", "cols", None, "depth"), P("rows", "cols", None, "depth"))
    return jax.shard_map(shards, mesh=mesh, in_specs=in_specs, out_specs=out_specs, check_vma=False)
```

```python
import math

import jax
import jax.numpy as jnp
from jax import lax
from jax.experimental import pallas as pl
from jax.experimental.pallas import tpu as pltpu
from jax.sharding import PartitionSpec as P


NB = 2048
RK = 64
BF = jnp.bfloat16
F32 = jnp.float32


def nt(first, second):
    return lax.dot_general(
        first, second, (((1,), (1,)), ((), ())), preferred_element_type=F32
    )


def nn(first, second):
    return lax.dot_general(
        first, second, (((1,), (0,)), ((), ())), preferred_element_type=F32
    )


def halves(x):
    high = x.astype(BF)
    return high, (x - high.astype(F32)).astype(BF)


def start_pair():
    rows = start_rows(RK, NB)
    high = lax.reduce_precision(rows, 8, 7)
    return jnp.concatenate([high, rows - high], axis=0).astype(BF)


def product(mul, first, second):
    a, b = halves(first), halves(second)
    return mul(a[0], b[0]) + (mul(a[0], b[1]) + mul(a[1], b[0]))


def start_rows(rank, width):
    freq = lax.broadcasted_iota(jnp.int32, (rank, width), 0) + 1
    cell = 2 * lax.broadcasted_iota(jnp.int32, (rank, width), 1) + 1
    phase = freq * cell % (4 * width)
    return jnp.cos(phase.astype(F32) * (math.pi / (2 * width)))


def spread(x, lane):
    return jnp.broadcast_to(x[:, lane : lane + 1], (8, 128))


def factor_inverse(full):
    v = [full[8 * b : 8 * b + 8] for b in range(8)]
    sub = lax.broadcasted_iota(jnp.int32, (8, 128), 0)
    out = []
    for b in range(8):
        at = 8 * b
        rows = [jnp.broadcast_to(v[b][p : p + 1], (8, 128)) for p in range(8)]
        s = [[spread(rows[p], at + q) for q in range(p + 1)] for p in range(8)]
        u = [[None] * 8 for _ in range(8)]
        last = b == 7
        block = None
        for p in range(8):
            y = lax.rsqrt(s[p][p])
            n = rows[p] * y
            t = n * y
            block = n if block is None else jnp.where(sub == p, n, block)
            low = {r: s[r][p] * y for r in range(p + 1, 8)}
            for q in range(p + 1, 8):
                for r in range(p + 1, q + 1):
                    s[q][r] = s[q][r] - low[q] * low[r]
                rows[q] = rows[q] - low[q] * n
            if not last:
                scaled = {r: low[r] * y for r in low}
                for q in range(p):
                    rows[q] = rows[q] - u[q][p] * t
                    for r in scaled:
                        u[q][r] = u[q][r] - u[q][p] * scaled[r]
                for r in scaled:
                    u[p][r] = scaled[r]
            rows[p] = t
        out.append(block)
        if not last:
            for below in range(b + 1, 8):
                c = [spread(v[below], at + q) * rows[q] for q in range(8)]
                v[below] = v[below] - (((c[0] + c[1]) + (c[2] + c[3])) + ((c[4] + c[5]) + (c[6] + c[7])))
    return jnp.concatenate(out, axis=0)


def masks():
    row = lax.broadcasted_iota(jnp.int32, (RK, 2 * RK), 0)
    col = lax.broadcasted_iota(jnp.int32, (RK, 2 * RK), 1)
    return row == col, row + RK == col, col >= RK


def store_gram(grams, at, gram):
    grams[0, at], grams[1, at] = halves(gram)


def gram_product(rows, grams, at):
    high, low = halves(rows)
    return nn(high, grams[0, at]) + (nn(high, grams[1, at]) + nn(low, grams[0, at]))


def inverse_rows(z, gz):
    diag, unit, upper = masks()
    gram = product(nt, z, jnp.concatenate([gz, jnp.zeros(gz.shape, F32)], axis=0))
    trace = jnp.sum(z * gz, keepdims=True)
    shift = 1e-05 * trace / RK + 1e-06
    full = jnp.where(diag, gram + shift, gram)
    full = jnp.where(unit, 1.0, full)
    return jnp.where(upper, factor_inverse(full), 0.0)


def sweeps(grams, z, z_ref, more_ref):
    n = z.shape[1]
    z_ref[...] = z
    more_ref[:, :n] = gram_product(z, grams, 1)

    @pl.loop(0, 4)
    def _(half):
        z, gz = z_ref[...], more_ref[:, :n]
        ahead = gram_product(gz, grams, half % 2)
        rows = jnp.concatenate([gz, ahead, z], axis=1)
        rows = product(nn, inverse_rows(z, gz), jnp.concatenate([rows, rows], axis=0))
        z_ref[...] = rows[:, :n]
        more_ref[...] = rows[:, n:]

    return more_ref[:, n:], z_ref[...]


def take(choice, copies):
    for holds, sources in choice:

        @pl.when(holds)
        def _():
            for src, (dst, sem) in zip(sources, copies):
                pltpu.make_async_copy(src, dst, sem).start()


def right_choice(pieces, first, second):
    block = jnp.where(first == 0, 0, jnp.where(first == 3, 1, first + 1))
    own, before, after, far = pieces
    return [
        (second == offset, [piece.at[block]])
        for offset, piece in ((0, own), (3, before), (1, after), (2, far))
    ]


def left_choice(pieces, more, panel, col):
    offset = (panel // 2 - col + 8) % 8
    spot = panel % 2
    return [
        (offset == o, [pieces[n].at[spot], more[n].at[spot]])
        for n, o in enumerate((0, 1, 2, 3, 5, 6, 7, 4))
    ]


def right_kernel(triples, place, tile_right, *refs):
    pieces_u, pieces_v, (r, picked, grams, first_right, sems) = refs[:4], refs[4:8], refs[8:]
    fixed = pltpu.make_async_copy(tile_right, first_right, sems.at[2, 0])
    fixed.start()
    waits = []
    for slot in range(6):
        panel = jnp.maximum(triples[slot], 0)
        dx = (panel % 4 - place[0] + 4) % 4
        dy = (panel // 4 - place[1] + 4) % 4
        copies = [(r.at[pl.ds(RK * slot, RK)], sems.at[0, slot]), (picked.at[slot], sems.at[1, slot])]
        take(right_choice(pieces_u, dx, dy), copies[:1])
        take(right_choice(pieces_v, dy, dx), copies[1:])
        waits += copies
    fixed.wait()
    r[384:448], r[448:512] = halves(first_right[...])
    for dst, sem in waits:
        pltpu.make_async_copy(pieces_u[0].at[0], dst, sem).wait()
    right = r[...]
    grams[0], grams[1] = halves(nt(right, right))


def right_side(triples, place, *arrays):
    smem = pl.BlockSpec(memory_space=pltpu.SMEM)
    vmem = pl.BlockSpec(memory_space=pltpu.VMEM)
    hbm = pl.BlockSpec(memory_space=pltpu.HBM)
    return pl.pallas_call(
        right_kernel,
        out_shape=[
            jax.ShapeDtypeStruct((512, NB), BF),
            jax.ShapeDtypeStruct((6, RK, NB), BF),
            jax.ShapeDtypeStruct((2, 512, 512), BF),
        ],
        in_specs=[smem, smem] + [hbm] * len(arrays),
        out_specs=[vmem] * 3,
        scratch_shapes=[pltpu.VMEM((RK, NB), F32), pltpu.SemaphoreType.DMA((3, 6))],
        compiler_params=pltpu.CompilerParams(vmem_limit_bytes=20 << 20),
        name="right_side",
    )(triples, place, *[pltpu.with_memory_space_constraint(x, pltpu.HBM) for x in arrays])


def layer_kernel(triples, place, r, inner_r, right_grams, tile_left, start, *refs):
    left_u, left_v = refs[:8], refs[8:16]
    probe, image, w, inner_l, d, first_left, begin, grams, z_ref, more_ref, sems = refs[16:]
    fixed = [
        pltpu.make_async_copy(src, dst, sems.at[2, n])
        for n, (src, dst) in enumerate(((tile_left, first_left), (start, begin)))
    ]
    for copy in fixed:
        copy.start()
    waits = []
    for slot in range(6):
        copies = [
            (w.at[pl.ds(RK * slot, RK)], sems.at[0, slot]),
            (inner_l.at[slot], sems.at[1, slot]),
        ]
        panel = jnp.maximum(triples[slot], 0)
        take(left_choice(left_u, left_v, panel, place[2]), copies)
        waits += copies
    for copy in fixed:
        copy.wait()
    w[384:448], w[448:512] = halves(first_left[...])
    grams[0, 1] = right_grams[0]
    grams[1, 1] = right_grams[1]
    row = lax.broadcasted_iota(jnp.int32, (128, 128), 0)
    col = lax.broadcasted_iota(jnp.int32, (128, 128), 1)
    d[...] = jnp.zeros_like(d)
    d[3] = jnp.where((row - col) % RK == 0, 0.5, 0.0).astype(BF)
    for slot in range(6):
        for dst, sem in waits[2 * slot : 2 * slot + 2]:
            pltpu.make_async_copy(left_u[0].at[0], dst, sem).wait()
        value = -nt(inner_r[slot], inner_l[slot])
        value = jnp.where(triples[slot] >= 0, value, jnp.zeros_like(value)).astype(BF)
        at = RK * (slot % 2)
        d[slot // 2, at : at + RK, at : at + RK] = value
    left = w[...]
    raw = nt(left, left)
    z = nt(begin[...], left)
    z = z[:RK] + z[RK:]
    mixed = []
    for t in range(4):
        high, low = halves(raw[128 * t : 128 * t + 128])
        mixed.append(nn(d[t], high) + nn(d[t], low))
    mixed = jnp.concatenate(mixed + [z], axis=0)
    high, low = halves(mixed)
    out = []
    for t in range(4):
        cut = slice(128 * t, 128 * t + 128)
        out.append(nt(high[:, cut], d[t]) + nt(low[:, cut], d[t]))
    out = jnp.concatenate(out, axis=1)
    store_gram(grams, 0, out[:512])
    x, y = sweeps(grams, out[512:], z_ref, more_ref)
    high, low = halves(x)
    out = []
    for t in range(4):
        cut = slice(128 * t, 128 * t + 128)
        out.append(nn(high[:, cut], d[t]) + nn(low[:, cut], d[t]))
    high, low = halves(jnp.concatenate(out, axis=1))
    probe[...] = nn(high, left) + nn(low, left)
    high, low = halves(y)
    right = r[...]
    image[...] = nn(high, right) + nn(low, right)


def layer_update(triples, place, right, *arrays):
    smem = pl.BlockSpec(memory_space=pltpu.SMEM)
    vmem = pl.BlockSpec(memory_space=pltpu.VMEM)
    hbm = pl.BlockSpec(memory_space=pltpu.HBM)
    return pl.pallas_call(
        layer_kernel,
        out_shape=[jax.ShapeDtypeStruct((RK, NB), F32)] * 2,
        in_specs=[smem, smem] + [vmem] * 3 + [hbm] * len(arrays),
        out_specs=[vmem, vmem],
        scratch_shapes=[
            pltpu.VMEM((512, NB), BF),
            pltpu.VMEM((6, RK, NB), BF),
            pltpu.VMEM((4, 128, 128), BF),
            pltpu.VMEM((RK, NB), F32),
            pltpu.VMEM((2 * RK, NB), BF),
            pltpu.VMEM((2, 2, 512, 512), BF),
            pltpu.VMEM((RK, 512), F32),
            pltpu.VMEM((RK, 1024), F32),
            pltpu.SemaphoreType.DMA((3, 6)),
        ],
        compiler_params=pltpu.CompilerParams(vmem_limit_bytes=40 << 20),
        name="layer_update",
    )(triples, place, *right, *[pltpu.with_memory_space_constraint(x, pltpu.HBM) for x in arrays])


def join_kernel(
    offset, probes_a, probes_b, images_a, images_b, start, new_left, new_right, w, r, grams, z_ref, more_ref
):
    for store, first, second in ((w, probes_a, probes_b), (r, images_a, images_b)):
        store[0:64], store[128:192] = halves(first[...])
        store[64:128], store[192:256] = halves(second[...])

    def folded(x):
        return (x[:128, :128] + x[128:, 128:]) + (x[:128, 128:] + x[128:, :128])

    left = w[...]
    right = r[...]
    z = nt(start[...], left)
    z = z[:RK] + z[RK:]
    z = z[:, :128] + z[:, 128:]
    store_gram(grams, 0, folded(nt(left, left)))
    store_gram(grams, 1, folded(nt(right, right)))
    x, y = sweeps(grams, z, z_ref, more_ref)
    share = new_left.shape[1]
    cut = pl.ds(pl.multiple_of(offset[0], share), share)
    for store, coefs, out, scale in (
        (w, x, new_left, math.sqrt(NB)),
        (r, y, new_right, 1.0 / math.sqrt(NB)),
    ):
        high, low = halves(coefs)
        out[...] = scale * (
            nn(high, store[0:128, cut])
            + (nn(high, store[128:256, cut]) + nn(low, store[0:128, cut]))
        )


def join(offset, probes_a, probes_b, images_a, images_b, start, share):
    vmem = pl.BlockSpec(memory_space=pltpu.VMEM)
    return pl.pallas_call(
        join_kernel,
        out_shape=[jax.ShapeDtypeStruct((RK, share), F32)] * 2,
        in_specs=[pl.BlockSpec(memory_space=pltpu.SMEM)] + [vmem] * 5,
        out_specs=[vmem, vmem],
        scratch_shapes=[
            pltpu.VMEM((256, NB), BF),
            pltpu.VMEM((256, NB), BF),
            pltpu.VMEM((2, 2, 128, 128), BF),
            pltpu.VMEM((RK, 128), F32),
            pltpu.VMEM((RK, 256), F32),
        ],
        compiler_params=pltpu.CompilerParams(vmem_limit_bytes=40 << 20),
        name="join",
    )(offset, probes_a, probes_b, images_a, images_b, start)


def move(x, dx, dy):
    route = []
    for r in range(16):
        y, x_at = divmod(r, 4)
        route.append((r, (y + dy) % 4 * 4 + (x_at + dx) % 4))
    return lax.ppermute(x, "rows", route)


def turn(x, step):
    return lax.ppermute(x, "cols", [(c, (c + step) % 8) for c in range(8)])


def line(x, along_x):
    step = (lambda k: move(x, k, 0)) if along_x else (lambda k: move(x, 0, k))
    found = [step(1), step(-1), step(2)]
    return jnp.stack([x] + found)


def plane(stack, along_x, way):
    step = (lambda v, k: move(v, k, 0)) if along_x else (lambda v, k: move(v, 0, k))
    before, after = step(stack, 1), step(stack, -1)
    return [stack, before, after, step(before if way > 0 else after, way)]


def ring(own, way):
    f1, b1 = turn(own, 1), turn(own, -1)
    f2, b2 = turn(f1, 1), turn(b1, -1)
    f3, b3 = turn(f2, 1), turn(b2, -1)
    return [own, b1, b2, b3, f3, f2, f1, turn(f3 if way > 0 else b3, way)]


def masked(rows, rank):
    index = lax.broadcasted_iota(jnp.int32, (RK, 1), 0)
    return jnp.where(index < rank, rows, 0)


def update(tile_left, tile_right, left_u, left_v, rank_left, right_u, right_v, rank_right, triples):
    row = lax.axis_index("rows")
    place = jnp.stack([row % 4, row // 4, lax.axis_index("cols")]).astype(jnp.int32)
    right_u = right_u[0, 0, 0]
    right_v = masked(right_v[0, 0, 0], rank_right[0, 0, 0])
    left_v = masked(left_v[0, :, 0], rank_left[0, :, 0][:, None, None])
    all_u = ring(left_u[0, :, 0], 1)
    all_v = ring(left_v, -1)
    pieces_u = plane(line(right_u, True), False, 1)
    pieces_v = plane(line(right_v, False), True, -1)
    tile_triples = triples[0, 0, 0]
    start = start_pair()
    right = right_side(tile_triples, place, tile_right[0, 0], *pieces_u, *pieces_v)
    probe, image = layer_update(
        tile_triples, place, right, tile_left[0, 0], start, *all_u, *all_v
    )
    layer = lax.axis_index("depth")
    other_probe, other_image = lax.ppermute((probe, image), "depth", [(0, 1), (1, 0)])
    share = NB // 2
    new_left, new_right = join(
        (layer * share).astype(jnp.int32).reshape(1),
        probe,
        other_probe,
        image,
        other_image,
        start,
        share,
    )
    return new_left.reshape(1, 1, RK, share), new_right.reshape(1, 1, RK, share)


def solution(mesh):
    in_specs = (
        P("rows", "cols", None, None),
        P("rows", "cols", None, None),
        P("depth", "cols", "rows", None, None),
        P("depth", "cols", "rows", None, None),
        P("depth", "cols", "rows"),
        P("depth", "rows", "cols", None, None),
        P("depth", "rows", "cols", None, None),
        P("depth", "rows", "cols"),
        P("rows", "cols", "depth", None),
    )
    out_specs = (P("rows", "cols", None, "depth"), P("rows", "cols", None, "depth"))
    return jax.shard_map(update, mesh=mesh, in_specs=in_specs, out_specs=out_specs, check_vma=False)
```
